32 devices in a mesh: tm: 16 (over z, x, core), space: 2 (over y).
Axes of the slice: x: 2, y: 2, z: 4, core: 2. Of those that a mesh axis runs over, the one named last changes fastest.
Arguments:
- conv_input: bfloat16 [16, 12, 40, 256], P('tm', None, 'space'), may hold values from -6 to 6
- conv_out: bfloat16 [16, 12, 40, 256], P('tm', None, 'space'), may hold values from -20 to 20
- kernel: bfloat16 [3, 3, 3, 256, 256], replicated, may hold values from -0.078125 to 0.078125
- gain: float32 [256], replicated, may hold values from 0.25 to 1.75
- bias: float32 [256], replicated, may hold values from -4 to 4
- cotangent: bfloat16 [16, 12, 40, 256], P('tm', None, 'space'), may hold values from -7 to 7
Outputs:
- grad_input: bfloat16 [16, 12, 40, 256], P('tm', None, 'space')
- grad_kernel: float32 [3, 3, 3, 256, 256], P(None, None, None, None, 'space')
- grad_gain: float32 [256], replicated
- grad_bias: float32 [256], replicated
The draws below stay inside these ranges and needn't reach their ends.
All inputs are finite; a program needn't handle non-finite values.
Results may differ from the reference program's by a relative error of at most 0.0075.
Values may be sent and summed in bfloat16 or wider, within the bound.
A program may use at most 64 MiB of HBM per device.

```python
import jax
import jax.numpy as jnp
from jax import lax

CH = 256
GROUPS = 32
ROWS = 12
COLS = 20
FRAMES = 16
WIDTH = 40


def ordered_levels(key, count, low, high):
    order = jax.random.permutation(key, count).astype(jnp.float32)
    return low + (high - low) * order / max(count - 1, 1)


def draw_conv_out(key, part):
    keys = jax.random.split(jax.random.fold_in(key, 7), 6)
    shape = (FRAMES, ROWS, WIDTH, CH)
    base = jnp.clip(jax.random.normal(keys[0], shape, jnp.float32), -3.5, 3.5)
    frame_scale = ordered_levels(keys[1], FRAMES, 0.6, 1.8)
    frame_offset = jax.random.uniform(keys[2], (FRAMES,), jnp.float32, -0.5, 0.5)
    strips = WIDTH // COLS
    strip_scale = jnp.exp(ordered_levels(keys[3], strips, -0.35, 0.35))
    column_scale = strip_scale[jnp.arange(WIDTH) // COLS]
    scales = jnp.exp(jax.random.uniform(keys[4], (CH,), jnp.float32, -0.6, 0.6))
    offsets = jnp.clip(0.5 * jax.random.normal(keys[5], (CH,), jnp.float32), -1.5, 1.5)
    values = base * frame_scale[:, None, None, None] * column_scale[None, None, :, None] * scales
    values = values + offsets + frame_offset[:, None, None, None]
    return jnp.clip(values, -20.0, 20.0).astype(jnp.bfloat16)


def draw_cotangent(key, part):
    keys = jax.random.split(jax.random.fold_in(key, 11), 3)
    shape = (FRAMES, ROWS, WIDTH, CH)
    base = jnp.clip(jax.random.normal(keys[0], shape, jnp.float32), -4.0, 4.0)
    channel_offset = jnp.clip(1.5 * jax.random.normal(keys[1], (CH,), jnp.float32), -2.0, 2.0)
    frame_factor = ordered_levels(keys[2], FRAMES, 0.4, 1.2)
    values = base + channel_offset * frame_factor[:, None, None, None]
    return jnp.clip(values, -7.0, 7.0).astype(jnp.bfloat16)


def block_levels(rng, extent, shards, least, top_value):
    def one(dim, blocks):
        draws = jax.random.uniform(jax.random.fold_in(jax.random.fold_in(rng, 6), dim), (blocks,), jnp.float32, least / len(shards), top_value / len(shards))
        return jnp.repeat(jnp.exp(draws), extent[dim] // blocks).reshape((-1,) + (1,) * (len(extent) - dim - 1))

    loudness = one(*shards[0])
    for cut in shards[1:]:
        loudness = loudness * one(*cut)
    return loudness


def noise(key, extent, deviation, reach, cuts=(), dtype=jnp.bfloat16):
    drawn = deviation * jax.random.normal(key, extent, jnp.float32)
    if cuts:
        drawn = drawn * block_levels(key, extent, cuts, -0.22, 0.18)
    return jnp.clip(drawn, -reach, reach).astype(dtype)


def setup_inputs(seed: int = 0) -> dict:
    key_of = jax.random.split(jax.random.key(seed), 7)
    conv_input = noise(key_of[0], (FRAMES, ROWS, WIDTH, CH), 1.0, 6.0, ((0, 16), (2, 2)))
    conv_out = draw_conv_out(jax.random.fold_in(key_of[6], 71), 0)
    kernel = noise(key_of[2], (3, 3, 3, CH, CH), (27 * CH) ** -0.5, 0.078125)
    gain = jnp.clip(1.0 + 0.15 * jax.random.normal(key_of[3], (CH,), jnp.float32), 0.25, 1.75)
    bias = noise(key_of[4], (CH,), 0.8, 4.0, (), jnp.float32)
    cotangent = draw_cotangent(jax.random.fold_in(key_of[6], 71), 0)
    return {"conv_input": conv_input, "conv_out": conv_out, "kernel": kernel, "gain": gain, "bias": bias, "cotangent": cotangent}


epsilon = 1e-06

def reference(conv_input, conv_out, kernel, gain, bias, cotangent):
    frames, rows, cols, chans = conv_out.shape
    width = chans // GROUPS
    grouped = conv_out.astype(jnp.float32).reshape(frames, rows, cols, GROUPS, width)
    count = frames * rows * cols * width
    mean = lax.optimization_barrier(jnp.sum(grouped, axis=(0, 1, 2, 4))) / count
    square = lax.optimization_barrier(jnp.sum(grouped * grouped, axis=(0, 1, 2, 4))) / count
    inv_std = lax.rsqrt(square - mean * mean + epsilon)
    normed_grouped = (grouped - mean[:, None]) * inv_std[:, None]
    normed = normed_grouped.reshape(frames, rows, cols, chans)
    shifted = normed * gain + bias
    sigma = jax.nn.sigmoid(shifted)
    grad_shift = cotangent.astype(jnp.float32) * sigma * (1.0 + shifted * (1.0 - sigma))
    grad_bias = lax.optimization_barrier(jnp.sum(grad_shift, axis=(0, 1, 2)))
    grad_gain = lax.optimization_barrier(jnp.sum(grad_shift * normed, axis=(0, 1, 2)))
    grad_grouped = (grad_shift * gain).reshape(frames, rows, cols, GROUPS, width)
    plain = lax.optimization_barrier(jnp.sum(grad_grouped, axis=(0, 1, 2, 4)))
    product = lax.optimization_barrier(jnp.sum(grad_grouped * normed_grouped, axis=(0, 1, 2, 4)))
    grad_conv = inv_std[:, None] * (grad_grouped - plain[:, None] / count - normed_grouped * product[:, None] / count)
    grad_conv = grad_conv.reshape(frames, rows, cols, chans).astype(jnp.bfloat16)
    padded_input = jnp.pad(conv_input, ((2, 0), (1, 1), (1, 1), (0, 0)))
    padded_grad = jnp.pad(grad_conv, ((0, 2), (1, 1), (1, 1), (0, 0)))
    flat_grad = grad_conv.reshape(-1, chans)
    taps = []
    accum = jnp.zeros((frames * rows * cols, chans), jnp.float32)
    for tap_t in range(3):
        for tap_h in range(3):
            for tap_w in range(3):
                source = padded_input[tap_t:tap_t + frames, tap_h:tap_h + rows, tap_w:tap_w + cols].reshape(-1, chans)
                taps.append(jnp.dot(source.T, flat_grad, preferred_element_type=jnp.float32))
                window = padded_grad[2 - tap_t:2 - tap_t + frames, 2 - tap_h:2 - tap_h + rows, 2 - tap_w:2 - tap_w + cols].reshape(-1, chans)
                accum = accum + jnp.dot(window, kernel[tap_t, tap_h, tap_w].T, preferred_element_type=jnp.float32)
    grad_kernel = jnp.stack(taps).reshape(3, 3, 3, chans, chans)
    grad_input = accum.reshape(frames, rows, cols, chans).astype(jnp.bfloat16)
    return (grad_input, grad_kernel, grad_gain, grad_bias)
```

```python
import functools

import jax
import jax.numpy as jnp
from jax import lax
from jax.experimental import pallas as pl
from jax.experimental.pallas import tpu as pltpu
from jax.sharding import PartitionSpec as P

GROUPS = 32
EPSILON = 1e-06
MESH = pl.DeviceIdType.MESH
F32 = jnp.float32
BF16 = jnp.bfloat16


def round_up(value, unit):
    return (value + unit - 1) // unit * unit


def group_sum(x, width):
    lanes = x.shape[1]
    lane = lax.broadcasted_iota(jnp.int32, x.shape, 1)
    step = 1
    while step < width:
        up = pltpu.roll(x, lanes - step, 1)
        down = pltpu.roll(x, step, 1)
        x = x + jnp.where((lane // step) % 2 == 0, up, down)
        step *= 2
    return x


def body(
    T, S, total_rows,
    x_ref, co_ref, k_ref, gain_ref, bias_ref, ct_ref,
    gi_ref, gk_ref, gg_ref, gb_ref,
    strip, edge_out, edge_in, slice_out, slice_in, x_in,
    st_out, st_in, fbuf, gown, gwide, xt, wbuf, acc, sbuf, rbuf,
    w_sem, st_send, st_recv, bulk_send, bulk_recv, rs_send, rs_recv,
):
    N = T * S
    _, rows, cols, chans = co_ref.shape
    ce = chans // S
    pitch = fbuf.shape[1]
    flat = rows * pitch
    flat_all = (rows + 2) * pitch
    halves = chans // 128
    t = lax.axis_index("tm")
    s = lax.axis_index("space")
    me = t * S + s

    load = pltpu.make_async_copy(k_ref, wbuf, w_sem)
    load.start()

    barrier = pltpu.get_barrier_semaphore()

    def greet(r, carry):
        d = lax.rem(me + r, N)
        pl.semaphore_signal(barrier, inc=1, device_id=(d // S, lax.rem(d, S)), device_id_type=MESH)
        return carry

    lax.fori_loop(1, N, greet, 0)

    for arr, ref in ((0, co_ref), (1, ct_ref)):
        whole = ref[0]
        for h in range(rows):
            edge_out[0, arr, h : h + 1, :] = whole[h, 0:1, :]
            edge_out[1, arr, h : h + 1, :] = whole[h, cols - 1 : cols, :]
        for j in range(S):
            slice_out[j, arr] = whole[:, :, j * ce : (j + 1) * ce]
    conv = co_ref[0].astype(F32)
    first = jnp.sum(jnp.sum(conv, axis=0), axis=0, keepdims=True)
    second = jnp.sum(jnp.sum(conv * conv, axis=0), axis=0, keepdims=True)

    def put_stats(which, one, two):
        for i in range(halves):
            st_out[which, i : i + 1, :] = one[:, i * 128 : (i + 1) * 128]
            st_out[which, halves + i : halves + i + 1, :] = two[:, i * 128 : (i + 1) * 128]

    def send_stats(which):
        def send(r, carry):
            d = lax.rem(me + r, N)
            pltpu.make_async_remote_copy(
                src_ref=st_out.at[which], dst_ref=st_in.at[which, r - 1],
                send_sem=st_send.at[which], recv_sem=st_recv.at[which],
                device_id=(d // S, lax.rem(d, S)), device_id_type=MESH,
            ).start()
            return carry

        lax.fori_loop(1, N, send, 0)

    def take_stats(which):
        pltpu.make_async_copy(st_in.at[which], st_in.at[which], st_recv.at[which]).wait()
        return jnp.sum(st_in[which], axis=0) + st_out[which]

    put_stats(0, first, second)
    pl.semaphore_wait(barrier, N - 1)
    send_stats(0)

    bulk = []

    def push(src, dst, device):
        i = len(bulk)
        copy = pltpu.make_async_remote_copy(
            src_ref=src, dst_ref=dst, send_sem=bulk_send.at[i], recv_sem=bulk_recv.at[i],
            device_id=device, device_id_type=MESH,
        )
        copy.start()
        bulk.append(copy)

    for k in range(3):
        tk = lax.rem(t + T - k, T)
        push(edge_out.at[1], edge_in.at[k, 0], (tk, lax.rem(s + 1, S)))
        push(edge_out.at[0], edge_in.at[k, 1], (tk, lax.rem(s + S - 1, S)))
        for r in range(1, S):
            other = lax.rem(s + S - r, S)
            push(slice_out.at[other], slice_in.at[k, r - 1], (tk, other))
    for r in range(1, S):
        push(x_ref.at[0], x_in.at[r - 1], (t, lax.rem(s + S - r, S)))
    for k in range(1, 3):
        tk = lax.rem(t + T - k, T)
        push(co_ref.at[0], strip.at[k - 1, 0], (tk, s))
        push(ct_ref.at[0], strip.at[k - 1, 1], (tk, s))

    fbuf[...] = jnp.zeros_like(fbuf)

    def put_input(index, value):
        fbuf[1 : rows + 1, 0:cols, :] = value.astype(F32)
        placed = fbuf[1 : rows + 1].reshape(flat, chans)
        xt[index] = jnp.transpose(placed).astype(BF16)

    put_input(0, x_ref[0])
    if total_rows > 27 * chans:
        acc[27 * chans :, :] = jnp.zeros((total_rows - 27 * chans, ce), F32)

    gain = gain_ref[...]
    bias = bias_ref[...]
    width = chans // GROUPS
    count = rows * cols * width * N
    sums = take_stats(0)
    grouped = group_sum(sums, width)
    mean2 = grouped[:halves] / count
    inv2 = lax.rsqrt(grouped[halves:] / count - mean2 * mean2 + EPSILON)

    def wide(two):
        return jnp.concatenate([two[i : i + 1] for i in range(halves)], axis=1)

    mean, inv = wide(mean2), wide(inv2)

    def shift_grad(conv, cot, mean, inv, gain, bias):
        normed = (conv.astype(F32) - mean) * inv
        shifted = normed * gain + bias
        sigma = jax.nn.sigmoid(shifted)
        return normed, cot.astype(F32) * sigma * (1.0 + shifted * (1.0 - sigma))

    normed, grad = shift_grad(co_ref[0], ct_ref[0], mean, inv, gain, bias)
    put_stats(
        1,
        jnp.sum(jnp.sum(grad, axis=0), axis=0, keepdims=True),
        jnp.sum(jnp.sum(grad * normed, axis=0), axis=0, keepdims=True),
    )
    send_stats(1)
    for copy in bulk:
        copy.wait_recv()
    for r in range(1, S):
        put_input(r, x_in[r - 1])
    sums = take_stats(1)
    chan_bias, chan_gain = wide(sums[:halves]), wide(sums[halves:])
    gb_ref[...] = chan_bias
    gg_ref[...] = chan_gain
    gain2 = jnp.concatenate([gain[:, i * 128 : (i + 1) * 128] for i in range(halves)], axis=0)
    plain = wide(group_sum(sums[:halves] * gain2, width)) / count
    product = wide(group_sum(sums[halves:] * gain2, width)) / count

    def conv_grad(conv, cot, params):
        mean, inv, gain, bias, plain, product = params
        normed, grad = shift_grad(conv, cot, mean, inv, gain, bias)
        return inv * (grad * gain - plain - normed * product)

    def part(v):
        out = v[..., 0:ce]
        for j in range(1, S):
            out = jnp.where(s == j, v[..., j * ce : (j + 1) * ce], out)
        return out

    params = (mean, inv, gain, bias, plain, product)
    own_params = tuple(part(p) for p in params)

    def shifts(f):
        n = f.shape[0]
        return (pltpu.roll(f, n - 1, 0), f, pltpu.roll(f, 1, 0))

    for k in range(3):
        live = t + k < T
        conv, cot = (co_ref[0], ct_ref[0]) if k == 0 else (strip[k - 1, 0], strip[k - 1, 1])
        g = jnp.where(live, conv_grad(conv, cot, params), 0.0)
        fbuf[1 : rows + 1, 0:cols, :] = g
        left = jnp.where(live & (s > 0), conv_grad(edge_in[k, 0, 0], edge_in[k, 0, 1], params), 0.0)
        right = jnp.where(live & (s < S - 1), conv_grad(edge_in[k, 1, 0], edge_in[k, 1, 1], params), 0.0)
        for h in range(rows):
            fbuf[h, pitch - 1 : pitch, :] = left[h : h + 1]
            fbuf[h + 1, cols : cols + 1, :] = right[h : h + 1]
        f = fbuf[...].reshape(flat_all, chans)
        for c, w in enumerate(shifts(f)):
            gown[k, :, c * chans : (c + 1) * chans] = w.astype(BF16)
            gwide[0, k, :, c * ce : (c + 1) * ce] = part(w).astype(BF16)
        near = [part(g)] + [
            jnp.where(live, conv_grad(slice_in[k, r - 1, 0], slice_in[k, r - 1, 1], own_params), 0.0)
            for r in range(1, S)
        ]
        for r in range(1, S):
            j = lax.rem(s + r, S)
            before, after = near[r - 1], near[(r + 1) % S]
            fbuf[1 : rows + 1, 0:cols, 0:ce] = near[r]
            fbuf[0:rows, pitch - 1 : pitch, 0:ce] = jnp.where(j > 0, before[:, cols - 1 : cols, :], 0.0)
            fbuf[1 : rows + 1, cols : cols + 1, 0:ce] = jnp.where(j < S - 1, after[:, 0:1, :], 0.0)
            f = fbuf[:, :, 0:ce].reshape(flat_all, ce)
            for c, w in enumerate(shifts(f)):
                gwide[r, k, :, c * ce : (c + 1) * ce] = w.astype(BF16)

    for a in range(3):
        for b in range(3):
            res = None
            for j in range(S):
                term = jnp.dot(
                    xt[j], gwide[j, 2 - a, (2 - b) * pitch : (2 - b) * pitch + flat, :],
                    preferred_element_type=F32,
                )
                res = term if res is None else res + term
            for c in range(3):
                at = ((a * 3 + b) * 3 + c) * chans
                acc[at : at + chans, :] = res[:, c * ce : (c + 1) * ce]

    bits = T.bit_length() - 1
    orders = [list(range(bits)), list(range(bits))]
    if bits > 2:
        orders[1][1], orders[1][2] = orders[1][2], orders[1][1]
    size = total_rows // 2
    offs = [0, 0]
    where = 0
    copies = []

    def side(bit):
        return lax.rem(t // (2**bit), 2)

    def partner(bit):
        return (t + (1 - 2 * side(bit)) * 2**bit, s)

    def span(p, off, n):
        return pl.ds(pl.multiple_of(p * size + off, 16), n)

    def begin(i, p):
        half = size >> (i + 1)
        start = size - (size >> i)
        bit = orders[p][i]
        mine = side(bit)
        sbuf[p, start : start + half, :] = acc[span(p, offs[p] + (1 - mine) * half, half), :].astype(BF16)
        copy = pltpu.make_async_remote_copy(
            src_ref=sbuf.at[p, start : start + half], dst_ref=rbuf.at[p, start : start + half],
            send_sem=rs_send.at[0, p, i], recv_sem=rs_recv.at[0, p, i],
            device_id=partner(bit), device_id_type=MESH,
        )
        copy.start()
        copies.append(copy)
        offs[p] = offs[p] + mine * half
        return copy

    def finish(i, p, copy):
        half = size >> (i + 1)
        start = size - (size >> i)
        copy.wait_recv()
        at = span(p, offs[p], half)
        acc[at, :] = acc[at, :] + rbuf[p, start : start + half, :].astype(F32)

    def input_grad(taps):
        total = None
        for a, b, c in taps:
            term = lax.dot_general(
                gown[2 - a, (2 - b) * pitch : (2 - b) * pitch + flat, c * chans : (c + 1) * chans],
                wbuf[a, b, c], (((1,), (1,)), ((), ())), preferred_element_type=F32,
            )
            total = term if total is None else total + term
        return total

    flying = [begin(0, 0), begin(0, 1)]
    for i in range(bits):
        for p in range(2):
            finish(i, p, flying[p])
            if i + 1 < bits:
                flying[p] = begin(i + 1, p)
        if i == 0:
            load.wait()
            every = [(a, b, c) for a in range(3) for b in range(3) for c in range(3)]
            total = input_grad(every).reshape(rows, pitch, chans)
            gi_ref[0] = total[:, 0:cols, :].astype(BF16)
    block = size >> bits
    for p in range(2):
        at = span(p, offs[p], block)
        gk_ref[at, :] = acc[at, :].astype(BF16)

    def spread(i, p):
        n = size >> (i + 1)
        bit = orders[p][i]
        at = span(p, offs[p], n)
        copy = pltpu.make_async_remote_copy(
            src_ref=gk_ref.at[at], dst_ref=gk_ref.at[at],
            send_sem=rs_send.at[1, p, i], recv_sem=rs_recv.at[1, p, i],
            device_id=partner(bit), device_id_type=MESH,
        )
        copy.start()
        copies.append(copy)
        offs[p] = offs[p] - side(bit) * n
        return copy

    flying = [spread(bits - 1, 0), spread(bits - 1, 1)]
    for i in reversed(range(bits)):
        for p in range(2):
            flying[p].wait_recv()
            if i > 0:
                flying[p] = spread(i - 1, p)

    for copy in copies:
        copy.wait_send()
    for copy in bulk:
        copy.wait_send()
    for which in range(2):
        pltpu.make_async_copy(st_in.at[which], st_in.at[which], st_send.at[which]).wait()


def solution(mesh):
    T, S = mesh.shape["tm"], mesh.shape["space"]

    def shards(conv_input, conv_out, kernel, gain, bias, cotangent):
        _, rows, cols, chans = conv_out.shape
        ce = chans // S
        bits = T.bit_length() - 1
        total_rows = round_up(27 * chans, 2 * T * 16)
        pitch = round_up(cols + 2, 16)
        n_bulk = 3 * (2 + S - 1) + (S - 1) + 4
        size = total_rows // 2
        vmem = pl.BlockSpec(memory_space=pltpu.VMEM)
        gi, gk, gg, gb = pl.pallas_call(
            functools.partial(body, T, S, total_rows),
            out_shape=(
                jax.ShapeDtypeStruct(conv_input.shape, BF16),
                jax.ShapeDtypeStruct((total_rows, ce), BF16),
                jax.ShapeDtypeStruct((1, chans), F32),
                jax.ShapeDtypeStruct((1, chans), F32),
            ),
            in_specs=[vmem, vmem, pl.BlockSpec(memory_space=pl.ANY), vmem, vmem, vmem],
            out_specs=(vmem, vmem, vmem, vmem),
            scratch_shapes=[
                pltpu.VMEM((2, 2, rows, cols, chans), BF16),
                pltpu.VMEM((2, 2, rows, chans), BF16),
                pltpu.VMEM((3, 2, 2, rows, chans), BF16),
                pltpu.VMEM((S, 2, rows, cols, ce), BF16),
                pltpu.VMEM((3, S - 1, 2, rows, cols, ce), BF16),
                pltpu.VMEM((S - 1, rows, cols, chans), BF16),
                pltpu.VMEM((2, 2 * chans // 128, 128), F32),
                pltpu.VMEM((2, T * S - 1, 2 * chans // 128, 128), F32),
                pltpu.VMEM((rows + 2, pitch, chans), F32),
                pltpu.VMEM((3, (rows + 2) * pitch, 3 * chans), BF16),
                pltpu.VMEM((S, 3, (rows + 2) * pitch, 3 * ce), BF16),
                pltpu.VMEM((S, chans, rows * pitch), BF16),
                pltpu.VMEM((3, 3, 3, chans, chans), BF16),
                pltpu.VMEM((total_rows, ce), F32),
                pltpu.VMEM((2, size, ce), BF16),
                pltpu.VMEM((2, size, ce), BF16),
                pltpu.SemaphoreType.DMA,
                pltpu.SemaphoreType.DMA((2,)),
                pltpu.SemaphoreType.DMA((2,)),
                pltpu.SemaphoreType.DMA((n_bulk,)),
                pltpu.SemaphoreType.DMA((n_bulk,)),
                pltpu.SemaphoreType.DMA((2, 2, bits)),
                pltpu.SemaphoreType.DMA((2, 2, bits)),
            ],
            compiler_params=pltpu.CompilerParams(
                collective_id=0, has_side_effects=True, vmem_limit_bytes=60 * 1024 * 1024
            ),
        )(conv_input, conv_out, kernel, gain.reshape(1, chans), bias.reshape(1, chans), cotangent)
        grad_kernel = gk[: 27 * chans].astype(F32).reshape(3, 3, 3, chans, ce)
        return gi, grad_kernel, gg.reshape(chans), gb.reshape(chans)

    strip = P("tm", None, "space", None)
    return jax.shard_map(
        shards,
        mesh=mesh,
        in_specs=(strip, strip, P(), P(), P(), strip),
        out_specs=(strip, P(None, None, None, None, "space"), P(), P()),
        check_vma=False,
    )
```

```python
import functools

import jax
import jax.numpy as jnp
from jax import lax
from jax.experimental import pallas as pl
from jax.experimental.pallas import tpu as pltpu
from jax.sharding import PartitionSpec as P

GROUPS = 32
STREAMS = 4
PARTS = 3
EPSILON = 1e-06
MESH = pl.DeviceIdType.MESH
F32 = jnp.float32
BF16 = jnp.bfloat16


def round_up(value, unit):
    return (value + unit - 1) // unit * unit


def group_sum(x, width):
    lanes = x.shape[1]
    lane = lax.broadcasted_iota(jnp.int32, x.shape, 1)
    step = 1
    while step < width:
        up = pltpu.roll(x, lanes - step, 1)
        down = pltpu.roll(x, step, 1)
        x = x + jnp.where((lane // step) % 2 == 0, up, down)
        step *= 2
    return x


def hand_out(gi_in, gk_in, gg_in, gb_in, gi_out, gk_out, gg_out, gb_out):
    gk_out[...] = gk_in[...].astype(F32)

    @pl.when(pl.program_id(0) == 0)
    def _():
        gi_out[...] = gi_in[...]
        gg_out[...] = gg_in[...]
        gb_out[...] = gb_in[...]


def body(
    T, S, sizes,
    x_hbm, co_hbm, k_ref, gain_ref, bias_ref, ct_hbm,
    gi_ref, gk_ref, gg_ref, gb_ref,
    x_ref, co_ref, ct_ref, strip, edge_out, edge_in, slice_out, slice_in, x_in,
    st_out, st_in, fbuf, gown, gwide, xt, wbuf, acc, sbuf, rbuf,
    in_sem, w_sem, st_send, st_recv, bulk_send, bulk_recv, rs_send, rs_recv,
):
    N = T * S
    total_rows = sum(sizes)
    _, rows, cols, chans = co_ref.shape
    ce = chans // S
    pitch = fbuf.shape[1]
    flat = rows * pitch
    flat_all = (rows + 2) * pitch
    halves = chans // 128
    t = lax.axis_index("tm")
    s = lax.axis_index("space")
    me = t * S + s

    loads = [
        pltpu.make_async_copy(src, dst, in_sem.at[i])
        for i, (src, dst) in enumerate(((co_hbm, co_ref), (ct_hbm, ct_ref), (x_hbm, x_ref)))
    ]
    for copy in loads:
        copy.start()
    load = pltpu.make_async_copy(k_ref, wbuf, w_sem)
    load.start()

    barrier = pltpu.get_barrier_semaphore()

    def greet(r, carry):
        d = lax.rem(me + r, N)
        pl.semaphore_signal(barrier, inc=1, device_id=(d // S, lax.rem(d, S)), device_id_type=MESH)
        return carry

    lax.fori_loop(1, N, greet, 0)

    for copy in loads:
        copy.wait()
    for arr, ref in ((0, co_ref), (1, ct_ref)):
        whole = ref[0]
        for h in range(rows):
            edge_out[0, arr, h : h + 1, :] = whole[h, 0:1, :]
            edge_out[1, arr, h : h + 1, :] = whole[h, cols - 1 : cols, :]
        for j in range(S):
            slice_out[j, arr] = whole[:, :, j * ce : (j + 1) * ce]
    conv = co_ref[0].astype(F32)
    first = jnp.sum(jnp.sum(conv, axis=0), axis=0, keepdims=True)
    second = jnp.sum(jnp.sum(conv * conv, axis=0), axis=0, keepdims=True)

    def put_stats(which, one, two):
        for i in range(halves):
            st_out[which, i : i + 1, :] = one[:, i * 128 : (i + 1) * 128]
            st_out[which, halves + i : halves + i + 1, :] = two[:, i * 128 : (i + 1) * 128]

    def send_stats(which):
        def send(r, carry):
            d = lax.rem(me + r, N)
            pltpu.make_async_remote_copy(
                src_ref=st_out.at[which], dst_ref=st_in.at[which, r - 1],
                send_sem=st_send.at[which], recv_sem=st_recv.at[which],
                device_id=(d // S, lax.rem(d, S)), device_id_type=MESH,
            ).start()
            return carry

        lax.fori_loop(1, N, send, 0)

    def take_stats(which):
        pltpu.make_async_copy(st_in.at[which], st_in.at[which], st_recv.at[which]).wait()
        return jnp.sum(st_in[which], axis=0) + st_out[which]

    put_stats(0, first, second)
    pl.semaphore_wait(barrier, N - 1)
    send_stats(0)

    bulk = []

    def push(src, dst, device):
        i = len(bulk)
        copy = pltpu.make_async_remote_copy(
            src_ref=src, dst_ref=dst, send_sem=bulk_send.at[i], recv_sem=bulk_recv.at[i],
            device_id=device, device_id_type=MESH,
        )
        copy.start()
        bulk.append(copy)

    for k in range(3):
        tk = lax.rem(t + T - k, T)
        push(edge_out.at[1], edge_in.at[k, 0], (tk, lax.rem(s + 1, S)))
        push(edge_out.at[0], edge_in.at[k, 1], (tk, lax.rem(s + S - 1, S)))
        for r in range(1, S):
            other = lax.rem(s + S - r, S)
            push(slice_out.at[other], slice_in.at[k, r - 1], (tk, other))
    for r in range(1, S):
        push(x_ref.at[0], x_in.at[r - 1], (t, lax.rem(s + S - r, S)))
    for k in range(1, 3):
        tk = lax.rem(t + T - k, T)
        push(co_ref.at[0], strip.at[k - 1, 0], (tk, s))
        push(ct_ref.at[0], strip.at[k - 1, 1], (tk, s))

    fbuf[...] = jnp.zeros_like(fbuf)

    def put_input(index, value):
        fbuf[1 : rows + 1, 0:cols, :] = value.astype(F32)
        placed = fbuf[1 : rows + 1].reshape(flat, chans)
        xt[index] = jnp.transpose(placed).astype(BF16)

    put_input(0, x_ref[0])
    if total_rows > 27 * chans:
        acc[27 * chans :, :] = jnp.zeros((total_rows - 27 * chans, ce), F32)

    gain = gain_ref[...]
    bias = bias_ref[...]
    width = chans // GROUPS
    count = rows * cols * width * N
    sums = take_stats(0)
    grouped = group_sum(sums, width)
    mean2 = grouped[:halves] / count
    inv2 = lax.rsqrt(grouped[halves:] / count - mean2 * mean2 + EPSILON)

    def wide(two):
        return jnp.concatenate([two[i : i + 1] for i in range(halves)], axis=1)

    mean, inv = wide(mean2), wide(inv2)

    def shift_grad(conv, cot, mean, inv, gain, bias):
        normed = (conv.astype(F32) - mean) * inv
        shifted = normed * gain + bias
        sigma = jax.nn.sigmoid(shifted)
        return normed, cot.astype(F32) * sigma * (1.0 + shifted * (1.0 - sigma))

    normed, grad = shift_grad(co_ref[0], ct_ref[0], mean, inv, gain, bias)
    put_stats(
        1,
        jnp.sum(jnp.sum(grad, axis=0), axis=0, keepdims=True),
        jnp.sum(jnp.sum(grad * normed, axis=0), axis=0, keepdims=True),
    )
    send_stats(1)
    for copy in bulk:
        copy.wait_recv()
    for r in range(1, S):
        put_input(r, x_in[r - 1])
    sums = take_stats(1)
    chan_bias, chan_gain = wide(sums[:halves]), wide(sums[halves:])
    gb_ref[...] = chan_bias
    gg_ref[...] = chan_gain
    gain2 = jnp.concatenate([gain[:, i * 128 : (i + 1) * 128] for i in range(halves)], axis=0)
    plain = wide(group_sum(sums[:halves] * gain2, width)) / count
    product = wide(group_sum(sums[halves:] * gain2, width)) / count

    def conv_grad(conv, cot, params):
        mean, inv, gain, bias, plain, product = params
        normed, grad = shift_grad(conv, cot, mean, inv, gain, bias)
        return inv * (grad * gain - plain - normed * product)

    def part(v):
        out = v[..., 0:ce]
        for j in range(1, S):
            out = jnp.where(s == j, v[..., j * ce : (j + 1) * ce], out)
        return out

    params = (mean, inv, gain, bias, plain, product)
    own_params = tuple(part(p) for p in params)

    def shifts(f):
        n = f.shape[0]
        return (pltpu.roll(f, n - 1, 0), f, pltpu.roll(f, 1, 0))

    for k in range(3):
        live = t + k < T
        conv, cot = (co_ref[0], ct_ref[0]) if k == 0 else (strip[k - 1, 0], strip[k - 1, 1])
        g = jnp.where(live, conv_grad(conv, cot, params), 0.0)
        fbuf[1 : rows + 1, 0:cols, :] = g
        left = jnp.where(live & (s > 0), conv_grad(edge_in[k, 0, 0], edge_in[k, 0, 1], params), 0.0)
        right = jnp.where(live & (s < S - 1), conv_grad(edge_in[k, 1, 0], edge_in[k, 1, 1], params), 0.0)
        for h in range(rows):
            fbuf[h, pitch - 1 : pitch, :] = left[h : h + 1]
            fbuf[h + 1, cols : cols + 1, :] = right[h : h + 1]
        f = fbuf[...].reshape(flat_all, chans)
        for c, w in enumerate(shifts(f)):
            gown[k, :, c * chans : (c + 1) * chans] = w.astype(BF16)
            gwide[0, k, :, c * ce : (c + 1) * ce] = part(w).astype(BF16)
        near = [part(g)] + [
            jnp.where(live, conv_grad(slice_in[k, r - 1, 0], slice_in[k, r - 1, 1], own_params), 0.0)
            for r in range(1, S)
        ]
        for r in range(1, S):
            j = lax.rem(s + r, S)
            before, after = near[r - 1], near[(r + 1) % S]
            fbuf[1 : rows + 1, 0:cols, 0:ce] = near[r]
            fbuf[0:rows, pitch - 1 : pitch, 0:ce] = jnp.where(j > 0, before[:, cols - 1 : cols, :], 0.0)
            fbuf[1 : rows + 1, cols : cols + 1, 0:ce] = jnp.where(j < S - 1, after[:, 0:1, :], 0.0)
            f = fbuf[:, :, 0:ce].reshape(flat_all, ce)
            for c, w in enumerate(shifts(f)):
                gwide[r, k, :, c * ce : (c + 1) * ce] = w.astype(BF16)

    bits = T.bit_length() - 1
    straight = list(range(bits))
    swapped = list(range(bits))
    if bits > 2:
        swapped[1], swapped[2] = swapped[2], swapped[1]
    streams = len(sizes)
    orders = [(straight, swapped)[p % 2] for p in range(streams)]
    bases = [sum(sizes[:p]) for p in range(streams)]
    offs = [0] * streams
    flying = [None] * streams
    copies = []

    def side(bit):
        return lax.rem(t // (2**bit), 2)

    def partner(bit):
        return (t + (1 - 2 * side(bit)) * 2**bit, s)

    def span(p, off, n):
        return pl.ds(pl.multiple_of(bases[p] + off, 16), n)

    def begin(i, p):
        half = sizes[p] >> (i + 1)
        start = bases[p] + sizes[p] - (sizes[p] >> i)
        bit = orders[p][i]
        mine = side(bit)
        sbuf[start : start + half, :] = acc[span(p, offs[p] + (1 - mine) * half, half), :].astype(BF16)
        copy = pltpu.make_async_remote_copy(
            src_ref=sbuf.at[start : start + half], dst_ref=rbuf.at[start : start + half],
            send_sem=rs_send.at[0, p, i], recv_sem=rs_recv.at[0, p, i],
            device_id=partner(bit), device_id_type=MESH,
        )
        copy.start()
        copies.append(copy)
        offs[p] = offs[p] + mine * half
        flying[p] = copy

    def finish(i, p):
        half = sizes[p] >> (i + 1)
        start = bases[p] + sizes[p] - (sizes[p] >> i)
        flying[p].wait_recv()
        at = span(p, offs[p], half)
        acc[at, :] = acc[at, :] + rbuf[start : start + half, :].astype(F32)

    def input_grad(a, total):
        for b in range(3):
            for c in range(3):
                term = lax.dot_general(
                    gown[2 - a, (2 - b) * pitch : (2 - b) * pitch + flat, c * chans : (c + 1) * chans],
                    wbuf[a, b, c], (((1,), (1,)), ((), ())), preferred_element_type=F32,
                )
                total = term if total is None else total + term
        return total

    started = 0
    for a in range(3):
        for b in range(3):
            res = None
            for j in range(S):
                term = jnp.dot(
                    xt[j], gwide[j, 2 - a, (2 - b) * pitch : (2 - b) * pitch + flat, :],
                    preferred_element_type=F32,
                )
                res = term if res is None else res + term
            for c in range(3):
                at = ((a * 3 + b) * 3 + c) * chans
                acc[at : at + chans, :] = res[:, c * ce : (c + 1) * ce]
            done = total_rows if a * 3 + b == 8 else ((a * 3 + b) * 3 + 3) * chans
            while started < streams and bases[started] + sizes[started] <= done:
                begin(0, started)
                started += 1

    load.wait()
    total = None
    for i in range(bits):
        for p in range(streams):
            finish(i, p)
            if i + 1 < bits:
                begin(i + 1, p)
        if i == 0:
            for a in range(3):
                total = input_grad(a, total)
            gi_ref[0] = total.reshape(rows, pitch, chans)[:, 0:cols, :].astype(BF16)

    def spread(i, p):
        n = sizes[p] >> (i + 1)
        bit = orders[p][i]
        at = span(p, offs[p], n)
        copy = pltpu.make_async_remote_copy(
            src_ref=gk_ref.at[at], dst_ref=gk_ref.at[at],
            send_sem=rs_send.at[1, p, i], recv_sem=rs_recv.at[1, p, i],
            device_id=partner(bit), device_id_type=MESH,
        )
        copy.start()
        copies.append(copy)
        offs[p] = offs[p] - side(bit) * n
        flying[p] = copy

    for p in range(streams):
        at = span(p, offs[p], sizes[p] >> bits)
        gk_ref[at, :] = acc[at, :].astype(BF16)
        spread(bits - 1, p)
    for i in reversed(range(bits)):
        for p in range(streams):
            flying[p].wait_recv()
            if i > 0:
                spread(i - 1, p)

    for copy in copies:
        copy.wait_send()
    for copy in bulk:
        copy.wait_send()
    for which in range(2):
        pltpu.make_async_copy(st_in.at[which], st_in.at[which], st_send.at[which]).wait()


def solution(mesh):
    T, S = mesh.shape["tm"], mesh.shape["space"]

    def shards(conv_input, conv_out, kernel, gain, bias, cotangent):
        _, rows, cols, chans = conv_out.shape
        ce = chans // S
        bits = T.bit_length() - 1
        groups = round_up(27 * chans, T * 16) // (T * 16)
        streams = min(STREAMS, groups)
        sizes = [(groups // streams + (p < groups % streams)) * T * 16 for p in range(streams)]
        total_rows = sum(sizes)
        pitch = round_up(cols + 2, 16)
        n_bulk = 3 * (2 + S - 1) + (S - 1) + 4
        vmem = pl.BlockSpec(memory_space=pltpu.VMEM)
        whole = pl.BlockSpec(memory_space=pl.ANY)
        gi, gk, gg, gb = pl.pallas_call(
            functools.partial(body, T, S, sizes),
            out_shape=(
                jax.ShapeDtypeStruct(conv_input.shape, BF16),
                jax.ShapeDtypeStruct((total_rows, ce), BF16),
                jax.ShapeDtypeStruct((1, chans), F32),
                jax.ShapeDtypeStruct((1, chans), F32),
            ),
            in_specs=[whole, whole, whole, vmem, vmem, whole],
            out_specs=(vmem, vmem, vmem, vmem),
            scratch_shapes=[
                pltpu.VMEM(conv_input.shape, BF16),
                pltpu.VMEM(conv_out.shape, BF16),
                pltpu.VMEM(cotangent.shape, BF16),
                pltpu.VMEM((2, 2, rows, cols, chans), BF16),
                pltpu.VMEM((2, 2, rows, chans), BF16),
                pltpu.VMEM((3, 2, 2, rows, chans), BF16),
                pltpu.VMEM((S, 2, rows, cols, ce), BF16),
                pltpu.VMEM((3, S - 1, 2, rows, cols, ce), BF16),
                pltpu.VMEM((S - 1, rows, cols, chans), BF16),
                pltpu.VMEM((2, 2 * chans // 128, 128), F32),
                pltpu.VMEM((2, T * S - 1, 2 * chans // 128, 128), F32),
                pltpu.VMEM((rows + 2, pitch, chans), F32),
                pltpu.VMEM((3, (rows + 2) * pitch, 3 * chans), BF16),
                pltpu.VMEM((S, 3, (rows + 2) * pitch, 3 * ce), BF16),
                pltpu.VMEM((S, chans, rows * pitch), BF16),
                pltpu.VMEM((3, 3, 3, chans, chans), BF16),
                pltpu.VMEM((total_rows, ce), F32),
                pltpu.VMEM((total_rows, ce), BF16),
                pltpu.VMEM((total_rows, ce), BF16),
                pltpu.SemaphoreType.DMA((3,)),
                pltpu.SemaphoreType.DMA,
                pltpu.SemaphoreType.DMA((2,)),
                pltpu.SemaphoreType.DMA((2,)),
                pltpu.SemaphoreType.DMA((n_bulk,)),
                pltpu.SemaphoreType.DMA((n_bulk,)),
                pltpu.SemaphoreType.DMA((2, streams, bits)),
                pltpu.SemaphoreType.DMA((2, streams, bits)),
            ],
            compiler_params=pltpu.CompilerParams(
                collective_id=0, has_side_effects=True, vmem_limit_bytes=60 * 1024 * 1024
            ),
        )(conv_input, conv_out, kernel, gain.reshape(1, chans), bias.reshape(1, chans), cotangent)
        part_rows = 27 * chans // PARTS
        gi, gk, gg, gb = pl.pallas_call(
            hand_out,
            grid=(PARTS,),
            out_shape=(
                jax.ShapeDtypeStruct(gi.shape, BF16),
                jax.ShapeDtypeStruct((27 * chans, ce), F32),
                jax.ShapeDtypeStruct((1, chans), F32),
                jax.ShapeDtypeStruct((1, chans), F32),
            ),
            in_specs=[
                pl.BlockSpec(gi.shape, lambda i: (0, 0, 0, 0)),
                pl.BlockSpec((part_rows, ce), lambda i: (i, 0)),
                pl.BlockSpec((1, chans), lambda i: (0, 0)),
                pl.BlockSpec((1, chans), lambda i: (0, 0)),
            ],
            out_specs=(
                pl.BlockSpec(gi.shape, lambda i: (0, 0, 0, 0)),
                pl.BlockSpec((part_rows, ce), lambda i: (i, 0)),
                pl.BlockSpec((1, chans), lambda i: (0, 0)),
                pl.BlockSpec((1, chans), lambda i: (0, 0)),
            ),
        )(gi, gk, gg, gb)
        return gi, gk.reshape(3, 3, 3, chans, ce), gg.reshape(chans), gb.reshape(chans)

    strip = P("tm", None, "space", None)
    return jax.shard_map(
        shards,
        mesh=mesh,
        in_specs=(strip, strip, P(), P(), P(), strip),
        out_specs=(strip, P(None, None, None, None, "space"), P(), P()),
        check_vma=False,
    )
```

```python
import functools

import jax
import jax.numpy as jnp
from jax import lax
from jax.experimental import pallas as pl
from jax.experimental.pallas import tpu as pltpu
from jax.sharding import PartitionSpec as P

GROUPS = 32
STREAMS = 6
PARTS = 2
EPSILON = 1e-06
MESH = pl.DeviceIdType.MESH
F32 = jnp.float32
BF16 = jnp.bfloat16


def round_up(value, unit):
    return (value + unit - 1) // unit * unit


def group_sum(x, width):
    lanes = x.shape[1]
    lane = lax.broadcasted_iota(jnp.int32, x.shape, 1)
    step = 1
    while step < width:
        up = pltpu.roll(x, lanes - step, 1)
        down = pltpu.roll(x, step, 1)
        x = x + jnp.where((lane // step) % 2 == 0, up, down)
        step *= 2
    return x


def hand_out(gi_in, gk_in, gg_in, gb_in, gi_out, gk_out, gg_out, gb_out):
    gk_out[...] = gk_in[...].astype(F32)

    @pl.when(pl.program_id(0) == 0)
    def _():
        gi_out[...] = gi_in[...]
        gg_out[...] = gg_in[...]
        gb_out[...] = gb_in[...]


def body(
    T, S, sizes,
    x_hbm, co_hbm, k_ref, gain_ref, bias_ref, ct_hbm,
    gi_ref, gk_ref, gg_ref, gb_ref,
    x_ref, co_ref, ct_ref, strip, edge_out, edge_in, slice_out, slice_in, x_in,
    st_out, st_in, fbuf, gown, gwide, xt, wbuf, acc, sbuf, rbuf,
    in_sem, w_sem, st_send, st_recv, bulk_send, bulk_recv, rs_send, rs_recv,
):
    N = T * S
    total_rows = sum(sizes)
    _, rows, cols, chans = co_ref.shape
    ce = chans // S
    pitch = fbuf.shape[1]
    flat = rows * pitch
    flat_all = (rows + 2) * pitch
    halves = chans // 128
    t = lax.axis_index("tm")
    s = lax.axis_index("space")
    me = t * S + s

    loads = [
        pltpu.make_async_copy(src, dst, in_sem.at[i])
        for i, (src, dst) in enumerate(((co_hbm, co_ref), (ct_hbm, ct_ref), (x_hbm, x_ref)))
    ]
    for copy in loads:
        copy.start()
    load = pltpu.make_async_copy(k_ref, wbuf, w_sem)
    load.start()

    barrier = pltpu.get_barrier_semaphore()

    def greet(r, carry):
        d = lax.rem(me + r, N)
        pl.semaphore_signal(barrier, inc=1, device_id=(d // S, lax.rem(d, S)), device_id_type=MESH)
        return carry

    lax.fori_loop(1, N, greet, 0)

    for copy in loads:
        copy.wait()
    for arr, ref in ((0, co_ref), (1, ct_ref)):
        whole = ref[0]
        for h in range(rows):
            edge_out[0, arr, h : h + 1, :] = whole[h, 0:1, :]
            edge_out[1, arr, h : h + 1, :] = whole[h, cols - 1 : cols, :]
        for j in range(S):
            slice_out[j, arr] = whole[:, :, j * ce : (j + 1) * ce]
    conv = co_ref[0].astype(F32)
    first = jnp.sum(jnp.sum(conv, axis=0), axis=0, keepdims=True)
    second = jnp.sum(jnp.sum(conv * conv, axis=0), axis=0, keepdims=True)

    def put_stats(which, one, two):
        for i in range(halves):
            st_out[which, i : i + 1, :] = one[:, i * 128 : (i + 1) * 128]
            st_out[which, halves + i : halves + i + 1, :] = two[:, i * 128 : (i + 1) * 128]

    def send_stats(which):
        def send(r, carry):
            r = 1 + lax.rem(r + N // 2 - 1, N - 1)
            d = lax.rem(me + r, N)
            pltpu.make_async_remote_copy(
                src_ref=st_out.at[which], dst_ref=st_in.at[which, r - 1],
                send_sem=st_send.at[which], recv_sem=st_recv.at[which],
                device_id=(d // S, lax.rem(d, S)), device_id_type=MESH,
            ).start()
            return carry

        lax.fori_loop(1, N, send, 0)

    def take_stats(which):
        pltpu.make_async_copy(st_in.at[which], st_in.at[which], st_recv.at[which]).wait()
        return jnp.sum(st_in[which], axis=0) + st_out[which]

    put_stats(0, first, second)
    pl.semaphore_wait(barrier, N - 1)
    send_stats(0)

    bulk = []

    def push(src, dst, device):
        i = len(bulk)
        copy = pltpu.make_async_remote_copy(
            src_ref=src, dst_ref=dst, send_sem=bulk_send.at[i], recv_sem=bulk_recv.at[i],
            device_id=device, device_id_type=MESH,
        )
        copy.start()
        bulk.append(copy)

    back = lax.rem(t + T - 1, T)
    for arr, ref in ((0, co_ref), (1, ct_ref)):
        push(ref.at[0], strip.at[0, arr], (back, s))
    for r in range(1, S):
        other = lax.rem(s + S - r, S)
        push(slice_out.at[other], slice_in.at[0, r - 1], (t, other))
    relayed = len(bulk)
    for k in range(3):
        tk = lax.rem(t + T - k, T)
        push(edge_out.at[1], edge_in.at[k, 0], (tk, lax.rem(s + 1, S)))
        push(edge_out.at[0], edge_in.at[k, 1], (tk, lax.rem(s + S - 1, S)))
    for r in range(1, S):
        push(x_ref.at[0], x_in.at[r - 1], (t, lax.rem(s + S - r, S)))
    direct = len(bulk)

    def relay_first():
        for arr in range(2):
            bulk[arr].wait_recv()
            push(strip.at[0, arr], strip.at[1, arr], (back, s))
        for r in range(1, S):
            bulk[1 + r].wait_recv()
            push(slice_in.at[0, r - 1], slice_in.at[1, r - 1], (back, s))

    def relay_second():
        for r in range(1, S):
            bulk[direct + 1 + r].wait_recv()
            push(slice_in.at[1, r - 1], slice_in.at[2, r - 1], (back, s))

    fbuf[...] = jnp.zeros_like(fbuf)

    def put_input(index, value):
        fbuf[1 : rows + 1, 0:cols, :] = value.astype(F32)
        placed = fbuf[1 : rows + 1].reshape(flat, chans)
        xt[index] = jnp.transpose(placed).astype(BF16)

    put_input(0, x_ref[0])
    if total_rows > 27 * chans:
        acc[27 * chans :, :] = jnp.zeros((total_rows - 27 * chans, ce), F32)

    gain = gain_ref[...]
    bias = bias_ref[...]
    width = chans // GROUPS
    count = rows * cols * width * N
    relay_first()
    sums = take_stats(0)
    grouped = group_sum(sums, width)
    mean2 = grouped[:halves] / count
    inv2 = lax.rsqrt(grouped[halves:] / count - mean2 * mean2 + EPSILON)

    def wide(two):
        return jnp.concatenate([two[i : i + 1] for i in range(halves)], axis=1)

    mean, inv = wide(mean2), wide(inv2)

    def shift_grad(conv, cot, mean, inv, gain, bias):
        normed = (conv.astype(F32) - mean) * inv
        shifted = normed * gain + bias
        sigma = jax.nn.sigmoid(shifted)
        return normed, cot.astype(F32) * sigma * (1.0 + shifted * (1.0 - sigma))

    normed, grad = shift_grad(co_ref[0], ct_ref[0], mean, inv, gain, bias)
    put_stats(
        1,
        jnp.sum(jnp.sum(grad, axis=0), axis=0, keepdims=True),
        jnp.sum(jnp.sum(grad * normed, axis=0), axis=0, keepdims=True),
    )
    send_stats(1)
    relay_second()
    for copy in bulk[relayed:direct]:
        copy.wait_recv()
    for r in range(1, S):
        put_input(r, x_in[r - 1])
    for copy in bulk[direct : direct + 2] + bulk[direct + 1 + S :]:
        copy.wait_recv()
    sums = take_stats(1)
    chan_bias, chan_gain = wide(sums[:halves]), wide(sums[halves:])
    gb_ref[...] = chan_bias
    gg_ref[...] = chan_gain
    gain2 = jnp.concatenate([gain[:, i * 128 : (i + 1) * 128] for i in range(halves)], axis=0)
    plain = wide(group_sum(sums[:halves] * gain2, width)) / count
    product = wide(group_sum(sums[halves:] * gain2, width)) / count

    def conv_grad(conv, cot, params):
        mean, inv, gain, bias, plain, product = params
        normed, grad = shift_grad(conv, cot, mean, inv, gain, bias)
        return inv * (grad * gain - plain - normed * product)

    def part(v):
        out = v[..., 0:ce]
        for j in range(1, S):
            out = jnp.where(s == j, v[..., j * ce : (j + 1) * ce], out)
        return out

    params = (mean, inv, gain, bias, plain, product)
    own_params = tuple(part(p) for p in params)

    def shifts(f):
        n = f.shape[0]
        return (pltpu.roll(f, n - 1, 0), f, pltpu.roll(f, 1, 0))

    for k in range(3):
        live = t + k < T
        conv, cot = (co_ref[0], ct_ref[0]) if k == 0 else (strip[k - 1, 0], strip[k - 1, 1])
        g = jnp.where(live, conv_grad(conv, cot, params), 0.0)
        fbuf[1 : rows + 1, 0:cols, :] = g
        left = jnp.where(live & (s > 0), conv_grad(edge_in[k, 0, 0], edge_in[k, 0, 1], params), 0.0)
        right = jnp.where(live & (s < S - 1), conv_grad(edge_in[k, 1, 0], edge_in[k, 1, 1], params), 0.0)
        for h in range(rows):
            fbuf[h, pitch - 1 : pitch, :] = left[h : h + 1]
            fbuf[h + 1, cols : cols + 1, :] = right[h : h + 1]
        f = fbuf[...].reshape(flat_all, chans)
        for c, w in enumerate(shifts(f)):
            gown[k, :, c * chans : (c + 1) * chans] = w.astype(BF16)
            gwide[0, k, :, c * ce : (c + 1) * ce] = part(w).astype(BF16)
        near = [part(g)] + [
            jnp.where(live, conv_grad(slice_in[k, r - 1, 0], slice_in[k, r - 1, 1], own_params), 0.0)
            for r in range(1, S)
        ]
        for r in range(1, S):
            j = lax.rem(s + r, S)
            before, after = near[r - 1], near[(r + 1) % S]
            fbuf[1 : rows + 1, 0:cols, 0:ce] = near[r]
            fbuf[0:rows, pitch - 1 : pitch, 0:ce] = jnp.where(j > 0, before[:, cols - 1 : cols, :], 0.0)
            fbuf[1 : rows + 1, cols : cols + 1, 0:ce] = jnp.where(j < S - 1, after[:, 0:1, :], 0.0)
            f = fbuf[:, :, 0:ce].reshape(flat_all, ce)
            for c, w in enumerate(shifts(f)):
                gwide[r, k, :, c * ce : (c + 1) * ce] = w.astype(BF16)

    bits = T.bit_length() - 1
    straight = list(range(bits))
    swapped = list(range(bits))
    if bits > 2:
        swapped[1], swapped[2] = swapped[2], swapped[1]
    streams = len(sizes)
    orders = [(straight, swapped)[p % 2] for p in range(streams)]
    bases = [sum(sizes[:p]) for p in range(streams)]
    offs = [0] * streams
    flying = [None] * streams
    copies = []

    def side(bit):
        return lax.rem(t // (2**bit), 2)

    def partner(bit):
        return (t + (1 - 2 * side(bit)) * 2**bit, s)

    def span(p, off, n):
        return pl.ds(pl.multiple_of(bases[p] + off, 16), n)

    def begin(i, p):
        half = sizes[p] >> (i + 1)
        start = bases[p] + sizes[p] - (sizes[p] >> i)
        bit = orders[p][i]
        mine = side(bit)
        sbuf[start : start + half, :] = acc[span(p, offs[p] + (1 - mine) * half, half), :].astype(BF16)
        copy = pltpu.make_async_remote_copy(
            src_ref=sbuf.at[start : start + half], dst_ref=rbuf.at[start : start + half],
            send_sem=rs_send.at[0, p, i], recv_sem=rs_recv.at[0, p, i],
            device_id=partner(bit), device_id_type=MESH,
        )
        copy.start()
        copies.append(copy)
        offs[p] = offs[p] + mine * half
        flying[p] = copy

    def finish(i, p):
        half = sizes[p] >> (i + 1)
        start = bases[p] + sizes[p] - (sizes[p] >> i)
        flying[p].wait_recv()
        at = span(p, offs[p], half)
        acc[at, :] = acc[at, :] + rbuf[start : start + half, :].astype(F32)

    def input_grad(a, total):
        for b in range(3):
            for c in range(3):
                term = lax.dot_general(
                    gown[2 - a, (2 - b) * pitch : (2 - b) * pitch + flat, c * chans : (c + 1) * chans],
                    wbuf[a, b, c], (((1,), (1,)), ((), ())), preferred_element_type=F32,
                )
                total = term if total is None else total + term
        return total

    started = 0
    for a in range(3):
        for b in range(3):
            res = None
            for j in range(S):
                term = jnp.dot(
                    xt[j], gwide[j, 2 - a, (2 - b) * pitch : (2 - b) * pitch + flat, :],
                    preferred_element_type=F32,
                )
                res = term if res is None else res + term
            for c in range(3):
                at = ((a * 3 + b) * 3 + c) * chans
                acc[at : at + chans, :] = res[:, c * ce : (c + 1) * ce]
            done = total_rows if a * 3 + b == 8 else ((a * 3 + b) * 3 + 3) * chans
            while started < streams and bases[started] + sizes[started] <= done:
                begin(0, started)
                started += 1

    load.wait()
    total = None
    for i in range(bits):
        for p in range(streams):
            finish(i, p)
            if i + 1 < bits:
                begin(i + 1, p)
        if i == 0:
            for a in range(3):
                total = input_grad(a, total)
            gi_ref[0] = total.reshape(rows, pitch, chans)[:, 0:cols, :].astype(BF16)

    def spread(i, p):
        n = sizes[p] >> (i + 1)
        bit = orders[p][i]
        at = span(p, offs[p], n)
        copy = pltpu.make_async_remote_copy(
            src_ref=gk_ref.at[at], dst_ref=gk_ref.at[at],
            send_sem=rs_send.at[1, p, i], recv_sem=rs_recv.at[1, p, i],
            device_id=partner(bit), device_id_type=MESH,
        )
        copy.start()
        copies.append(copy)
        offs[p] = offs[p] - side(bit) * n
        flying[p] = copy

    for p in range(streams):
        at = span(p, offs[p], sizes[p] >> bits)
        gk_ref[at, :] = acc[at, :].astype(BF16)
        spread(bits - 1, p)
    for i in reversed(range(bits)):
        for p in range(streams):
            flying[p].wait_recv()
            if i > 0:
                spread(i - 1, p)

    for copy in copies:
        copy.wait_send()
    for copy in bulk:
        copy.wait_send()
    for which in range(2):
        pltpu.make_async_copy(st_in.at[which], st_in.at[which], st_send.at[which]).wait()


def solution(mesh):
    T, S = mesh.shape["tm"], mesh.shape["space"]

    def shards(conv_input, conv_out, kernel, gain, bias, cotangent):
        _, rows, cols, chans = conv_out.shape
        ce = chans // S
        bits = T.bit_length() - 1
        groups = round_up(27 * chans, T * 16) // (T * 16)
        streams = min(STREAMS, groups)
        sizes = [(groups // streams + (p < groups % streams)) * T * 16 for p in range(streams)]
        total_rows = sum(sizes)
        pitch = round_up(cols + 2, 16)
        n_bulk = 3 * (2 + S - 1) + (S - 1) + 4
        vmem = pl.BlockSpec(memory_space=pltpu.VMEM)
        whole = pl.BlockSpec(memory_space=pl.ANY)
        gi, gk, gg, gb = pl.pallas_call(
            functools.partial(body, T, S, sizes),
            out_shape=(
                jax.ShapeDtypeStruct(conv_input.shape, BF16),
                jax.ShapeDtypeStruct((total_rows, ce), BF16),
                jax.ShapeDtypeStruct((1, chans), F32),
                jax.ShapeDtypeStruct((1, chans), F32),
            ),
            in_specs=[whole, whole, whole, vmem, vmem, whole],
            out_specs=(vmem, vmem, vmem, vmem),
            scratch_shapes=[
                pltpu.VMEM(conv_input.shape, BF16),
                pltpu.VMEM(conv_out.shape, BF16),
                pltpu.VMEM(cotangent.shape, BF16),
                pltpu.VMEM((2, 2, rows, cols, chans), BF16),
                pltpu.VMEM((2, 2, rows, chans), BF16),
                pltpu.VMEM((3, 2, 2, rows, chans), BF16),
                pltpu.VMEM((S, 2, rows, cols, ce), BF16),
                pltpu.VMEM((3, S - 1, 2, rows, cols, ce), BF16),
                pltpu.VMEM((S - 1, rows, cols, chans), BF16),
                pltpu.VMEM((2, 2 * chans // 128, 128), F32),
                pltpu.VMEM((2, T * S - 1, 2 * chans // 128, 128), F32),
                pltpu.VMEM((rows + 2, pitch, chans), F32),
                pltpu.VMEM((3, (rows + 2) * pitch, 3 * chans), BF16),
                pltpu.VMEM((S, 3, (rows + 2) * pitch, 3 * ce), BF16),
                pltpu.VMEM((S, chans, rows * pitch), BF16),
                pltpu.VMEM((3, 3, 3, chans, chans), BF16),
                pltpu.VMEM((total_rows, ce), F32),
                pltpu.VMEM((total_rows, ce), BF16),
                pltpu.VMEM((total_rows, ce), BF16),
                pltpu.SemaphoreType.DMA((3,)),
                pltpu.SemaphoreType.DMA,
                pltpu.SemaphoreType.DMA((2,)),
                pltpu.SemaphoreType.DMA((2,)),
                pltpu.SemaphoreType.DMA((n_bulk,)),
                pltpu.SemaphoreType.DMA((n_bulk,)),
                pltpu.SemaphoreType.DMA((2, streams, bits)),
                pltpu.SemaphoreType.DMA((2, streams, bits)),
            ],
            compiler_params=pltpu.CompilerParams(
                collective_id=0, has_side_effects=True, vmem_limit_bytes=60 * 1024 * 1024
            ),
        )(conv_input, conv_out, kernel, gain.reshape(1, chans), bias.reshape(1, chans), cotangent)
        part_rows = 27 * chans // PARTS
        gi, gk, gg, gb = pl.pallas_call(
            hand_out,
            grid=(PARTS,),
            out_shape=(
                jax.ShapeDtypeStruct(gi.shape, BF16),
                jax.ShapeDtypeStruct((27 * chans, ce), F32),
                jax.ShapeDtypeStruct((1, chans), F32),
                jax.ShapeDtypeStruct((1, chans), F32),
            ),
            in_specs=[
                pl.BlockSpec(gi.shape, lambda i: (0, 0, 0, 0)),
                pl.BlockSpec((part_rows, ce), lambda i: (i, 0)),
                pl.BlockSpec((1, chans), lambda i: (0, 0)),
                pl.BlockSpec((1, chans), lambda i: (0, 0)),
            ],
            out_specs=(
                pl.BlockSpec(gi.shape, lambda i: (0, 0, 0, 0)),
                pl.BlockSpec((part_rows, ce), lambda i: (i, 0)),
                pl.BlockSpec((1, chans), lambda i: (0, 0)),
                pl.BlockSpec((1, chans), lambda i: (0, 0)),
            ),
        )(gi, gk, gg, gb)
        return gi, gk.reshape(3, 3, 3, chans, ce), gg.reshape(chans), gb.reshape(chans)

    strip = P("tm", None, "space", None)
    return jax.shard_map(
        shards,
        mesh=mesh,
        in_specs=(strip, strip, P(), P(), P(), strip),
        out_specs=(strip, P(None, None, None, None, "space"), P(), P()),
        check_vma=False,
    )
```
